1024 devices in a mesh: lat: 64 (over z, x), azim: 16 (over y, core).
Axes of the slice: x: 4, y: 8, z: 16, core: 2. Of those that a mesh axis runs over, the one named last changes fastest.
Arguments:
- magnetic: float32 [3, 32, 2048, 2048], P(None, None, 'lat', 'azim'), may hold values from -6 to 6
- kept_modes: int32 [2048], replicated, may hold values from 1 to 1024, as said below
Outputs:
- current_density: float32 [3, 32, 2048, 2048], P(None, None, 'lat', 'azim')
The draws below stay inside these ranges and needn't reach their ends.
Inputs may be any that keep to these rules, and one draw needn't show every extreme that they name: `kept_modes`: at latitude 2048 // 2 all 1024 modes are kept.
All inputs are finite; a program needn't handle non-finite values.
Results may differ from the reference program's by a relative error of at most 0.000068.
Values sent between devices are 32-bit elements; how exact they have to be, the bound alone decides.
A program may use at most 32 MiB of HBM per device.

```python
import math
import jax
import jax.numpy as jnp
from jax import lax

LONGITUDE_COUNT = 2048
RADII = 32
NTH = 2048


def draw_kept_modes(key, part):
    lat_ids = jnp.arange(NTH, dtype=jnp.int32)
    nearest = jnp.minimum(lat_ids, NTH - 1 - lat_ids)
    base_count = jnp.maximum(1, LONGITUDE_COUNT // 2 * 2 * nearest // NTH)
    jitter = jax.random.randint(jax.random.fold_in(key, 1), (NTH,), 0, 1 << 20, dtype=jnp.int32) % (base_count // 2 + 1)
    tally_counts = jnp.maximum(1, base_count - jitter)
    half_places = max(1, NTH // 512)
    polar_reach = max(1, NTH // 8)
    north = jax.random.randint(jax.random.fold_in(key, 2), (half_places,), 0, polar_reach, dtype=jnp.int32)
    south = NTH - 1 - jax.random.randint(jax.random.fold_in(key, 3), (half_places,), 0, polar_reach, dtype=jnp.int32)
    spots = jnp.concatenate([north, south])
    flurry_counts = jax.random.randint(jax.random.fold_in(key, 4), (2 * half_places,), LONGITUDE_COUNT // 4, LONGITUDE_COUNT // 2 + 1, dtype=jnp.int32)
    matched_flag = lat_ids[:, None] == spots[None, :]
    flurry_local = jnp.max(jnp.where(matched_flag, flurry_counts[None, :], 0), axis=1)
    tally_counts = jnp.where(flurry_local > 0, flurry_local, tally_counts)
    return jnp.where(lat_ids == NTH // 2, LONGITUDE_COUNT // 2, tally_counts).astype(jnp.int32)


def levels(own_key, dims, split, low, high):
    level = 1.0
    for position, shards_of in split:
        steps = jax.random.uniform(jax.random.fold_in(jax.random.fold_in(own_key, 6), position), (shards_of,), jnp.float32, low / len(split), high / len(split))
        level = level * jnp.repeat(jnp.exp(steps), dims[position] // shards_of).reshape((-1,) + (1,) * (len(dims) - 1 - position))
    return level


def scatter_about(key, dims, scale, most, split=(), held_as=jnp.bfloat16):
    gain = levels(key, dims, split, -0.22, 0.18) if split else 1.0
    drawn = jax.random.normal(key, dims, jnp.float32) * scale * gain
    return jnp.minimum(jnp.maximum(drawn, -most), most).astype(held_as)


def setup_inputs(seed: int = 0) -> dict:
    arg_keys = jax.random.split(jax.random.key(seed), 3)
    return {
        "magnetic": scatter_about(arg_keys[0], (3, RADII, NTH, LONGITUDE_COUNT), 1.0, 6.0, ((2, 64), (3, 16)), jnp.float32),
        "kept_modes": draw_kept_modes(jax.random.fold_in(arg_keys[2], 71), 0),
    }


inner_radius = 0.7
stencil_coeffs = (-1.0 / 60.0, 3.0 / 20.0, -3.0 / 4.0, 0.0, 3.0 / 4.0, -3.0 / 20.0, 1.0 / 60.0)


def central_diff(values, split_axis):
    length = values.shape[split_axis]
    widths = [(0, 0)] * values.ndim
    widths[split_axis] = (3, 3)
    padded = jnp.pad(values, widths)
    total = jnp.zeros_like(values)
    for offset in range(-3, 4):
        if offset != 0:
            total = total + stencil_coeffs[offset + 3] * lax.slice_in_dim(padded, 3 + offset, 3 + offset + length, axis=split_axis)
    return total


def reference(magnetic, kept_modes):
    spacing = math.pi / NTH
    colatitude = (jnp.arange(NTH, dtype=jnp.float32) + 0.5) * spacing
    radius = inner_radius + (jnp.arange(RADII, dtype=jnp.float32) + 0.5) * spacing
    radius = radius[:, None, None]
    inv_sin = (1.0 / jnp.sin(colatitude))[None, :, None]
    cotangent = (jnp.cos(colatitude) / jnp.sin(colatitude))[None, :, None]
    b_radial = magnetic[0]
    b_polar = magnetic[1]
    b_azim = magnetic[2]
    spectrum = jnp.fft.rfft(magnetic[:2], axis=-1)
    mode_ids = jnp.arange(LONGITUDE_COUNT // 2 + 1, dtype=jnp.int32)
    keep = mode_ids[None, :] < kept_modes[:, None]
    factor = jnp.where(keep, mode_ids[None, :], 0).astype(jnp.float32)
    azimuthal = jnp.fft.irfft(1j * factor[None, None, :, :] * spectrum, n=LONGITUDE_COUNT, axis=-1).astype(jnp.float32)
    j_radial = (central_diff(b_azim, 1) + spacing * cotangent * b_azim - spacing * inv_sin * azimuthal[1]) / radius
    j_polar = (spacing * inv_sin * azimuthal[0] - central_diff(radius * b_azim, 0)) / radius
    j_azim = (central_diff(radius * b_polar, 0) - central_diff(b_radial, 1)) / radius
    return jnp.stack([j_radial, j_polar, j_azim])
```

```python
import functools
import math

import jax
import jax.numpy as jnp
import numpy as np
from jax import lax
from jax.experimental import pallas as pl
from jax.experimental.pallas import tpu as pltpu
from jax.sharding import PartitionSpec as P

MESH = pl.DeviceIdType.MESH
F32 = jnp.float32
BF16 = jnp.bfloat16

inner_radius = 0.7
stencil_coeffs = (-1.0 / 60.0, 3.0 / 20.0, -3.0 / 4.0, 0.0, 3.0 / 4.0, -3.0 / 20.0, 1.0 / 60.0)
OFFSETS = (-3, -2, -1, 1, 2, 3)

RAD = 32
BAND = 32
SEG = 128
AZ = 16
HALF = BAND // AZ
ROWS = 2 * RAD
PADR = 3 * BAND


def mode_tables():
    a = np.arange(128)[:, None]
    b = np.arange(32)[:, None]
    q = np.arange(SEG)[None, :]
    p = np.arange(AZ)[:, None]
    high = 2.0 * np.pi * ((a * q) % 64) / 64.0
    twist = 2.0 * np.pi * ((b * q) % 2048) / 2048.0
    low = 2.0 * np.pi * ((p * b.T) % 16) / 16.0
    first = np.concatenate([np.cos(high), np.sin(high)], axis=1)
    second = np.stack([np.cos(twist), np.sin(twist)])
    third = np.stack([np.cos(low), np.sin(low)])
    third = np.pad(third, ((0, 0), (0, 0), (0, 96)))
    return first.astype(np.float32), second.astype(np.float32), third.astype(np.float32)


def split(value):
    high = value.astype(BF16)
    return high, (value - high.astype(F32)).astype(BF16)


def send_order():
    order = []
    for chips in (4, 3, -3, 2, -2, 1, -1, 0):
        for core in (0, 1):
            order.append((chips, core))
    return order


def kernel(
    lat_total,
    x4, x3, kept_hbm, latsc_hbm, radsc_hbm, tab1, tab2, tab3,
    out,
    kept, latsc, radsc, xs, ext, xt, rcv, whi, wlo, fhi, flo, acc, ret, az, outv, cot, gen,
    in_sem, small_sem, fsend, frecv, rsend, rrecv, hsend, hrecv, out_sem,
):
    lat = lax.axis_index("lat")
    me = lax.axis_index("azim")
    lats = lax.axis_size("lat")
    chip = me // 2
    core = me % 2
    north = (lat + lats - 1) % lats
    south = (lat + 1) % lats

    loads = [
        pltpu.make_async_copy(x3.at[0:2], xs.at[:, PADR : PADR + RAD * BAND, :], in_sem.at[0]),
        pltpu.make_async_copy(x4.at[0], ext.at[0, 3 : 3 + RAD, 8 : 8 + BAND, :], in_sem.at[1]),
        pltpu.make_async_copy(x4.at[2], ext.at[1, 3 : 3 + RAD, 8 : 8 + BAND, :], in_sem.at[2]),
    ]
    smalls = [
        pltpu.make_async_copy(kept_hbm, kept, small_sem.at[0]),
        pltpu.make_async_copy(latsc_hbm, latsc, small_sem.at[1]),
        pltpu.make_async_copy(radsc_hbm, radsc, small_sem.at[2]),
    ]
    for copy in loads + smalls:
        copy.start()

    barrier = pltpu.get_barrier_semaphore()
    for step in range(1, AZ):
        pl.semaphore_signal(barrier, inc=1, device_id={"azim": (me + step) % AZ}, device_id_type=MESH)
    pl.semaphore_signal(barrier, inc=1, device_id={"lat": north}, device_id_type=MESH)
    pl.semaphore_signal(barrier, inc=1, device_id={"lat": south}, device_id_type=MESH)
    loads[0].wait()
    pl.semaphore_wait(barrier, AZ + 1)

    peers = []
    for chips, flip in send_order():
        peer = ((chip + chips + 8) % 8) * 2 + (core + flip) % 2
        peers.append((peer, chips == 0 and flip == 0))
    forward = []
    for half in range(HALF):
        for peer, own in peers:
            row = peer + AZ * half
            for c in range(2):
                for k in range(RAD // 8):
                    xt[row, c * RAD + 8 * k : c * RAD + 8 * k + 8, :] = xs[
                        c, pl.ds(PADR + 8 * k * BAND + row, 8, stride=BAND), :
                    ]
            if own:
                pltpu.make_async_copy(xt.at[row], rcv.at[half, me], frecv.at[half, me]).start()
            else:
                copy = pltpu.make_async_remote_copy(
                    src_ref=xt.at[row],
                    dst_ref=rcv.at[half, me],
                    send_sem=fsend.at[half, peer],
                    recv_sem=frecv.at[half, me],
                    device_id={"azim": peer},
                    device_id_type=MESH,
                )
                copy.start()
                forward.append(copy)

    loads[1].wait()
    loads[2].wait()
    halos = [
        pltpu.make_async_remote_copy(
            src_ref=ext.at[:, 3 : 3 + RAD, BAND : BAND + 8, :],
            dst_ref=ext.at[:, 3 : 3 + RAD, 0:8, :],
            send_sem=hsend.at[0],
            recv_sem=hrecv.at[0],
            device_id={"lat": south},
            device_id_type=MESH,
        ),
        pltpu.make_async_remote_copy(
            src_ref=ext.at[:, 3 : 3 + RAD, 8:16, :],
            dst_ref=ext.at[:, 3 : 3 + RAD, 8 + BAND : 16 + BAND, :],
            send_sem=hsend.at[1],
            recv_sem=hrecv.at[1],
            device_id={"lat": north},
            device_id_type=MESH,
        ),
    ]
    for copy in halos:
        copy.start()
    for copy in smalls:
        copy.wait()

    base = lat * BAND + me
    side = lax.broadcasted_iota(jnp.int32, (HALF * 32, 128), 0)
    a = lax.broadcasted_iota(jnp.int32, (HALF * 32, 128), 1)
    mode = 32 * a + side % 32
    first_half = side < 32
    limit = jnp.where(first_half, kept[base], kept[base + AZ])
    scale = jnp.where(first_half, latsc[base], latsc[base + AZ])
    weight = jnp.where(mode < limit, mode, 0).astype(F32) * (2.0 / (AZ * SEG)) * scale
    sums = jnp.dot(weight, tab1[...], precision=lax.Precision.HIGHEST, preferred_element_type=F32)
    for half in range(HALF):
        c_sum = sums[32 * half : 32 * half + 32, 0:SEG]
        s_sum = sums[32 * half : 32 * half + 32, SEG : 2 * SEG]
        tc = tab2[0]
        ts = tab2[1]
        zero = jnp.zeros((96, SEG), F32)
        real = jnp.concatenate([c_sum * tc - s_sum * ts, zero], axis=0)
        imag = jnp.concatenate([s_sum * tc + c_sum * ts, zero], axis=0)
        gen[half] = -(
            jnp.dot(tab3[0], imag, precision=lax.Precision.HIGHEST, preferred_element_type=F32)
            + jnp.dot(tab3[1], real, precision=lax.Precision.HIGHEST, preferred_element_type=F32)
        )
    for half in range(HALF):
        for p in range(AZ):
            pair = jnp.concatenate(
                [gen[half, (p + AZ - 1) % AZ : (p + AZ - 1) % AZ + 1, :], gen[half, p : p + 1, :]], axis=1
            )
            turned = pltpu.roll(jnp.broadcast_to(pair, (SEG, 2 * SEG)), 0, 1, stride=1, stride_axis=0)
            high, low = split(turned[:, SEG:])
            for tile in range(8):
                for i in range(2):
                    for j in range(2):
                        if (j - i - 2 * tile - p) % AZ == 0:
                            at = (half, tile, slice(SEG * i, SEG * i + SEG), slice(SEG * j, SEG * j + SEG))
                            whi[at] = high
                            wlo[at] = low

    zeros = jnp.zeros((3, BAND, SEG), F32)
    ext[1, 0:3, 8 : 8 + BAND, :] = zeros
    ext[1, 3 + RAD : 6 + RAD, 8 : 8 + BAND, :] = zeros
    xs[1, 0:PADR, :] = jnp.zeros((PADR, SEG), F32)
    xs[1, PADR + RAD * BAND : 2 * PADR + RAD * BAND, :] = jnp.zeros((PADR, SEG), F32)
    for t in range(BAND):
        cot[t : t + 1, :] = jnp.full((1, SEG), latsc[lat_total + lat * BAND + t], F32)
    for copy in halos:
        copy.wait_recv()

    def stencils(r, carry):
        for c in range(2):
            top = ext[c, r + 3, 0:8, :]
            ext[c, r + 3, 0:8, :] = jnp.where(lat == 0, jnp.zeros_like(top), top)
            end = ext[c, r + 3, 8 + BAND : 16 + BAND, :]
            ext[c, r + 3, 8 + BAND : 16 + BAND, :] = jnp.where(lat == lats - 1, jnp.zeros_like(end), end)
        inverse = radsc[64 + r]
        th_r = jnp.zeros((BAND, SEG), F32)
        th_p = jnp.zeros((BAND, SEG), F32)
        dr_t = jnp.zeros((BAND, SEG), F32)
        dr_p = jnp.zeros((BAND, SEG), F32)
        for o in OFFSETS:
            weight_o = stencil_coeffs[o + 3]
            th_r = th_r + weight_o * ext[0, r + 3, 8 + o : 8 + o + BAND, :]
            th_p = th_p + weight_o * ext[1, r + 3, 8 + o : 8 + o + BAND, :]
            scaled = weight_o * radsc[r + 3 + o]
            dr_t = dr_t + scaled * xs[1, pl.ds(pl.multiple_of((r + 3 + o) * BAND, BAND), BAND), :]
            dr_p = dr_p + scaled * ext[1, r + 3 + o, 8 : 8 + BAND, :]
        outv[0, r] = (th_p + cot[...] * ext[1, r + 3, 8 : 8 + BAND, :]) * inverse
        outv[1, r] = -dr_p * inverse
        outv[2, r] = (dr_t - th_r) * inverse
        return carry

    def convert_and_apply(half):
        for source in range(AZ):
            pltpu.make_async_copy(xt.at[0], rcv.at[half, source], frecv.at[half, source]).wait()
        for source in range(AZ):
            high, low = split(rcv[half, source])
            lanes = slice(SEG * (source % 2), SEG * (source % 2) + SEG)
            for wrap in range(2):
                rows = slice(ROWS * (source // 2 + 8 * wrap), ROWS * (source // 2 + 8 * wrap) + ROWS)
                fhi[rows, lanes] = high
                flo[rows, lanes] = low
        acc[...] = jnp.zeros_like(acc)

        def tile_step(tile, carry):
            rows = pl.ds(pl.multiple_of(tile * ROWS, ROWS), 8 * ROWS)
            f_high = fhi[rows, :]
            f_low = flo[rows, :]
            w_high = whi[half, tile]
            acc[...] += (
                jnp.dot(f_high, w_high, preferred_element_type=F32)
                + jnp.dot(f_high, wlo[half, tile], preferred_element_type=F32)
                + jnp.dot(f_low, w_high, preferred_element_type=F32)
            )
            return carry

        lax.fori_loop(0, 8, tile_step, 0)
        for block in range(AZ):
            ret[half, block] = acc[
                ROWS * (block // 2) : ROWS * (block // 2) + ROWS, SEG * (block % 2) : SEG * (block % 2) + SEG
            ]
        sent = []
        for peer, own in peers:
            target = az.at[pl.ds(pl.multiple_of((me + AZ * half) * ROWS, ROWS), ROWS), :]
            if own:
                pltpu.make_async_copy(ret.at[half, peer], target, rrecv.at[half, me]).start()
            else:
                copy = pltpu.make_async_remote_copy(
                    src_ref=ret.at[half, peer],
                    dst_ref=target,
                    send_sem=rsend.at[half, peer],
                    recv_sem=rrecv.at[half, me],
                    device_id={"azim": peer},
                    device_id_type=MESH,
                )
                copy.start()
                sent.append(copy)
        return sent

    def finish(half):
        for source in range(AZ):
            t = source + AZ * half
            pltpu.make_async_copy(
                ret.at[half, 0], az.at[t * ROWS : t * ROWS + ROWS, :], rrecv.at[half, source]
            ).wait()

        def combine(r, carry):
            inverse = radsc[64 + r]
            for k in range(AZ // 8):
                t = AZ * half + 8 * k
                azim_r = az[pl.ds(t * ROWS + r, 8, stride=ROWS), :]
                azim_t = az[pl.ds(t * ROWS + RAD + r, 8, stride=ROWS), :]
                outv[0, r, t : t + 8, :] = outv[0, r, t : t + 8, :] - azim_t * inverse
                outv[1, r, t : t + 8, :] = outv[1, r, t : t + 8, :] + azim_r * inverse
            return carry

        lax.fori_loop(0, RAD, combine, 0)
        where = (slice(0, 2), slice(None), slice(AZ * half, AZ * half + AZ), slice(None))
        copy = pltpu.make_async_copy(outv.at[where], out.at[where], out_sem.at[half])
        copy.start()
        return copy

    lax.fori_loop(0, RAD, stencils, 0)
    written = [pltpu.make_async_copy(outv.at[2], out.at[2], out_sem.at[2])]
    written[0].start()
    back = []
    for half in range(HALF):
        back += convert_and_apply(half)
    for half in range(HALF):
        written.append(finish(half))
    for copy in forward + back + halos:
        copy.wait_send()
    for copy in written:
        copy.wait()


def solution(mesh):
    lat_total = BAND * mesh.shape["lat"]
    spacing = math.pi / lat_total
    theta = (np.arange(lat_total, dtype=np.float32) + np.float32(0.5)) * np.float32(spacing)
    theta = theta.astype(np.float64)
    lat_scalars = np.concatenate([spacing / np.sin(theta), spacing * np.cos(theta) / np.sin(theta)]).astype(np.float32)
    radius = inner_radius + (np.arange(RAD) + 0.5) * spacing
    rad_scalars = np.zeros(128, np.float32)
    rad_scalars[3 : 3 + RAD] = radius
    rad_scalars[64 : 64 + RAD] = 1.0 / radius
    first, second, third = mode_tables()

    def on_device(magnetic, kept_modes):
        flat = magnetic.reshape(3, RAD * BAND, SEG)
        anywhere = pl.BlockSpec(memory_space=pl.ANY)
        in_vmem = pl.BlockSpec(memory_space=pltpu.VMEM)
        dma = pltpu.SemaphoreType.DMA
        return pl.pallas_call(
            functools.partial(kernel, lat_total),
            out_shape=jax.ShapeDtypeStruct(magnetic.shape, F32),
            in_specs=[anywhere] * 5 + [in_vmem] * 3,
            out_specs=anywhere,
            scratch_shapes=[
                pltpu.SMEM((lat_total,), jnp.int32),
                pltpu.SMEM((2 * lat_total,), F32),
                pltpu.SMEM((128,), F32),
                pltpu.VMEM((2, 2 * PADR + RAD * BAND, SEG), F32),
                pltpu.VMEM((2, RAD + 6, BAND + 16, SEG), F32),
                pltpu.VMEM((BAND, ROWS, SEG), F32),
                pltpu.VMEM((HALF, AZ, ROWS, SEG), F32),
                pltpu.VMEM((HALF, 8, 2 * SEG, 2 * SEG), BF16),
                pltpu.VMEM((HALF, 8, 2 * SEG, 2 * SEG), BF16),
                pltpu.VMEM((16 * ROWS, 2 * SEG), BF16),
                pltpu.VMEM((16 * ROWS, 2 * SEG), BF16),
                pltpu.VMEM((8 * ROWS, 2 * SEG), F32),
                pltpu.VMEM((HALF, AZ, ROWS, SEG), F32),
                pltpu.VMEM((BAND * ROWS, SEG), F32),
                pltpu.VMEM((3, RAD, BAND, SEG), F32),
                pltpu.VMEM((BAND, SEG), F32),
                pltpu.VMEM((HALF, AZ, SEG), F32),
                dma((3,)),
                dma((3,)),
                dma((HALF, AZ)),
                dma((HALF, AZ)),
                dma((HALF, AZ)),
                dma((HALF, AZ)),
                dma((2,)),
                dma((2,)),
                dma((3,)),
            ],
            compiler_params=pltpu.CompilerParams(
                collective_id=0, has_side_effects=True, vmem_limit_bytes=40 * 1024 * 1024
            ),
        )(
            magnetic, flat, kept_modes, jnp.asarray(lat_scalars), jnp.asarray(rad_scalars),
            jnp.asarray(first), jnp.asarray(second), jnp.asarray(third),
        )

    return jax.shard_map(
        on_device,
        mesh=mesh,
        in_specs=(P(None, None, "lat", "azim"), P()),
        out_specs=P(None, None, "lat", "azim"),
        check_vma=False,
    )
```

```python
import functools
import math

import jax
import jax.numpy as jnp
import numpy as np
from jax import lax
from jax.experimental import pallas as pl
from jax.experimental.pallas import tpu as pltpu
from jax.sharding import PartitionSpec as P

MESH = pl.DeviceIdType.MESH
F32 = jnp.float32
BF16 = jnp.bfloat16

inner_radius = 0.7
stencil_coeffs = (-1.0 / 60.0, 3.0 / 20.0, -3.0 / 4.0, 0.0, 3.0 / 4.0, -3.0 / 20.0, 1.0 / 60.0)
OFFSETS = (-3, -2, -1, 1, 2, 3)

RAD = 32
BAND = 32
SEG = 128
AZ = 16
HALF = BAND // AZ
ROWS = 2 * RAD
PADR = 3 * BAND


def mode_tables():
    a = np.arange(128)[:, None]
    b = np.arange(32)[:, None]
    q = np.arange(SEG)[None, :]
    p = np.arange(AZ)[:, None]
    high = 2.0 * np.pi * ((a * q) % 64) / 64.0
    twist = 2.0 * np.pi * ((b * q) % 2048) / 2048.0
    low = 2.0 * np.pi * ((p * b.T) % 16) / 16.0
    first = np.concatenate([np.cos(high), np.sin(high)], axis=1)
    second = np.stack([np.cos(twist), np.sin(twist)])
    third = np.stack([np.cos(low), np.sin(low)])
    third = np.pad(third, ((0, 0), (0, 0), (0, 96)))
    return first.astype(np.float32), second.astype(np.float32), third.astype(np.float32)


def split(value):
    high = value.astype(BF16)
    return high, (value - high.astype(F32)).astype(BF16)


def send_order():
    order = []
    for chips in (4, 3, -3, 2, -2, 1, -1, 0):
        for core in (0, 1):
            order.append((chips, core))
    return order


def kernel(
    lat_total,
    x4, x3, kept_hbm, latsc_hbm, radsc_hbm, tab1_hbm, tab2_hbm, tab3_hbm,
    outv,
    kept, latsc, radsc, tab1, tab2, tab3, xs, ext, xt, rcv, whi, wlo, fhi, flo, acc, ret, az, cot, gen,
    in_sem, small_sem, fsend, frecv, rsend, rrecv, hsend, hrecv,
):
    lat = lax.axis_index("lat")
    me = lax.axis_index("azim")
    lats = lax.axis_size("lat")
    chip = me // 2
    core = me % 2
    north = (lat + lats - 1) % lats
    south = (lat + 1) % lats

    loads = [
        pltpu.make_async_copy(x3.at[0:2], xs.at[:, PADR : PADR + RAD * BAND, :], in_sem.at[0]),
        pltpu.make_async_copy(x4.at[0], ext.at[0, 3 : 3 + RAD, 8 : 8 + BAND, :], in_sem.at[1]),
        pltpu.make_async_copy(x4.at[2], ext.at[1, 3 : 3 + RAD, 8 : 8 + BAND, :], in_sem.at[2]),
    ]
    smalls = [
        pltpu.make_async_copy(kept_hbm, kept, small_sem.at[0]),
        pltpu.make_async_copy(latsc_hbm, latsc, small_sem.at[1]),
        pltpu.make_async_copy(radsc_hbm, radsc, small_sem.at[2]),
        pltpu.make_async_copy(tab1_hbm, tab1, small_sem.at[3]),
        pltpu.make_async_copy(tab2_hbm, tab2, small_sem.at[4]),
        pltpu.make_async_copy(tab3_hbm, tab3, small_sem.at[5]),
    ]
    for copy in loads + smalls:
        copy.start()

    barrier = pltpu.get_barrier_semaphore()
    for step in range(1, AZ):
        pl.semaphore_signal(barrier, inc=1, device_id={"azim": (me + step) % AZ}, device_id_type=MESH)
    pl.semaphore_signal(barrier, inc=1, device_id={"lat": north}, device_id_type=MESH)
    pl.semaphore_signal(barrier, inc=1, device_id={"lat": south}, device_id_type=MESH)
    loads[0].wait()
    pl.semaphore_wait(barrier, AZ + 1)

    peers = []
    for chips, flip in send_order():
        peer = ((chip + chips + 8) % 8) * 2 + (core + flip) % 2
        peers.append((peer, chips == 0 and flip == 0))
    forward = []
    for half in range(HALF):
        for peer, own in peers:
            row = peer + AZ * half
            for c in range(2):
                for k in range(RAD // 8):
                    xt[row, c * RAD + 8 * k : c * RAD + 8 * k + 8, :] = xs[
                        c, pl.ds(PADR + 8 * k * BAND + row, 8, stride=BAND), :
                    ]
            if own:
                pltpu.make_async_copy(xt.at[row], rcv.at[half, me], frecv.at[half, me]).start()
            else:
                copy = pltpu.make_async_remote_copy(
                    src_ref=xt.at[row],
                    dst_ref=rcv.at[half, me],
                    send_sem=fsend.at[half, peer],
                    recv_sem=frecv.at[half, me],
                    device_id={"azim": peer},
                    device_id_type=MESH,
                )
                copy.start()
                forward.append(copy)

    loads[1].wait()
    loads[2].wait()
    halos = [
        pltpu.make_async_remote_copy(
            src_ref=ext.at[:, 3 : 3 + RAD, BAND : BAND + 8, :],
            dst_ref=ext.at[:, 3 : 3 + RAD, 0:8, :],
            send_sem=hsend.at[0],
            recv_sem=hrecv.at[0],
            device_id={"lat": south},
            device_id_type=MESH,
        ),
        pltpu.make_async_remote_copy(
            src_ref=ext.at[:, 3 : 3 + RAD, 8:16, :],
            dst_ref=ext.at[:, 3 : 3 + RAD, 8 + BAND : 16 + BAND, :],
            send_sem=hsend.at[1],
            recv_sem=hrecv.at[1],
            device_id={"lat": north},
            device_id_type=MESH,
        ),
    ]
    for copy in halos:
        copy.start()
    for copy in smalls:
        copy.wait()

    base = lat * BAND + me
    side = lax.broadcasted_iota(jnp.int32, (HALF * 32, 128), 0)
    a = lax.broadcasted_iota(jnp.int32, (HALF * 32, 128), 1)
    mode = 32 * a + side % 32
    first_half = side < 32
    limit = jnp.where(first_half, kept[base], kept[base + AZ])
    scale = jnp.where(first_half, latsc[base], latsc[base + AZ])
    weight = jnp.where(mode < limit, mode, 0).astype(F32) * (2.0 / (AZ * SEG)) * scale
    sums = jnp.dot(weight, tab1[...], precision=lax.Precision.HIGHEST, preferred_element_type=F32)
    for half in range(HALF):
        c_sum = sums[32 * half : 32 * half + 32, 0:SEG]
        s_sum = sums[32 * half : 32 * half + 32, SEG : 2 * SEG]
        tc = tab2[0]
        ts = tab2[1]
        zero = jnp.zeros((96, SEG), F32)
        real = jnp.concatenate([c_sum * tc - s_sum * ts, zero], axis=0)
        imag = jnp.concatenate([s_sum * tc + c_sum * ts, zero], axis=0)
        gen[half] = -(
            jnp.dot(tab3[0], imag, precision=lax.Precision.HIGHEST, preferred_element_type=F32)
            + jnp.dot(tab3[1], real, precision=lax.Precision.HIGHEST, preferred_element_type=F32)
        )
    for half in range(HALF):
        for p in range(AZ):
            pair = jnp.concatenate(
                [gen[half, (p + AZ - 1) % AZ : (p + AZ - 1) % AZ + 1, :], gen[half, p : p + 1, :]], axis=1
            )
            turned = pltpu.roll(jnp.broadcast_to(pair, (SEG, 2 * SEG)), 0, 1, stride=1, stride_axis=0)
            high, low = split(turned[:, SEG:])
            for tile in range(8):
                for i in range(2):
                    for j in range(2):
                        if (j - i - 2 * tile - p) % AZ == 0:
                            at = (half, tile, slice(SEG * i, SEG * i + SEG), slice(SEG * j, SEG * j + SEG))
                            whi[at] = high
                            wlo[at] = low

    zeros = jnp.zeros((3, BAND, SEG), F32)
    ext[1, 0:3, 8 : 8 + BAND, :] = zeros
    ext[1, 3 + RAD : 6 + RAD, 8 : 8 + BAND, :] = zeros
    xs[1, 0:PADR, :] = jnp.zeros((PADR, SEG), F32)
    xs[1, PADR + RAD * BAND : 2 * PADR + RAD * BAND, :] = jnp.zeros((PADR, SEG), F32)
    for t in range(BAND):
        cot[t : t + 1, :] = jnp.full((1, SEG), latsc[lat_total + lat * BAND + t], F32)
    for copy in halos:
        copy.wait_recv()

    def stencils(r, carry):
        for c in range(2):
            top = ext[c, r + 3, 0:8, :]
            ext[c, r + 3, 0:8, :] = jnp.where(lat == 0, jnp.zeros_like(top), top)
            end = ext[c, r + 3, 8 + BAND : 16 + BAND, :]
            ext[c, r + 3, 8 + BAND : 16 + BAND, :] = jnp.where(lat == lats - 1, jnp.zeros_like(end), end)
        inverse = radsc[64 + r]
        th_r = jnp.zeros((BAND, SEG), F32)
        th_p = jnp.zeros((BAND, SEG), F32)
        dr_t = jnp.zeros((BAND, SEG), F32)
        dr_p = jnp.zeros((BAND, SEG), F32)
        for o in OFFSETS:
            weight_o = stencil_coeffs[o + 3]
            th_r = th_r + weight_o * ext[0, r + 3, 8 + o : 8 + o + BAND, :]
            th_p = th_p + weight_o * ext[1, r + 3, 8 + o : 8 + o + BAND, :]
            scaled = weight_o * radsc[r + 3 + o]
            dr_t = dr_t + scaled * xs[1, pl.ds(pl.multiple_of((r + 3 + o) * BAND, BAND), BAND), :]
            dr_p = dr_p + scaled * ext[1, r + 3 + o, 8 : 8 + BAND, :]
        outv[0, r] = (th_p + cot[...] * ext[1, r + 3, 8 : 8 + BAND, :]) * inverse
        outv[1, r] = -dr_p * inverse
        outv[2, r] = (dr_t - th_r) * inverse
        return carry

    def convert_and_apply(half):
        for source in range(AZ):
            pltpu.make_async_copy(xt.at[0], rcv.at[half, source], frecv.at[half, source]).wait()
        for source in range(AZ):
            high, low = split(rcv[half, source])
            lanes = slice(SEG * (source % 2), SEG * (source % 2) + SEG)
            for wrap in range(2):
                rows = slice(ROWS * (source // 2 + 8 * wrap), ROWS * (source // 2 + 8 * wrap) + ROWS)
                fhi[rows, lanes] = high
                flo[rows, lanes] = low
        acc[...] = jnp.zeros_like(acc)

        def tile_step(tile, carry):
            rows = pl.ds(pl.multiple_of(tile * ROWS, ROWS), 8 * ROWS)
            f_high = fhi[rows, :]
            f_low = flo[rows, :]
            w_high = whi[half, tile]
            acc[...] += (
                jnp.dot(f_high, w_high, preferred_element_type=F32)
                + jnp.dot(f_high, wlo[half, tile], preferred_element_type=F32)
                + jnp.dot(f_low, w_high, preferred_element_type=F32)
            )
            return carry

        lax.fori_loop(0, 8, tile_step, 0)
        for block in range(AZ):
            ret[half, block] = acc[
                ROWS * (block // 2) : ROWS * (block // 2) + ROWS, SEG * (block % 2) : SEG * (block % 2) + SEG
            ]
        sent = []
        for peer, own in peers:
            target = az.at[pl.ds(pl.multiple_of((me + AZ * half) * ROWS, ROWS), ROWS), :]
            if own:
                pltpu.make_async_copy(ret.at[half, peer], target, rrecv.at[half, me]).start()
            else:
                copy = pltpu.make_async_remote_copy(
                    src_ref=ret.at[half, peer],
                    dst_ref=target,
                    send_sem=rsend.at[half, peer],
                    recv_sem=rrecv.at[half, me],
                    device_id={"azim": peer},
                    device_id_type=MESH,
                )
                copy.start()
                sent.append(copy)
        return sent

    def finish(half):
        for source in range(AZ):
            t = source + AZ * half
            pltpu.make_async_copy(
                ret.at[half, 0], az.at[t * ROWS : t * ROWS + ROWS, :], rrecv.at[half, source]
            ).wait()

        def combine(r, carry):
            inverse = radsc[64 + r]
            for k in range(AZ // 8):
                t = AZ * half + 8 * k
                azim_r = az[pl.ds(t * ROWS + r, 8, stride=ROWS), :]
                azim_t = az[pl.ds(t * ROWS + RAD + r, 8, stride=ROWS), :]
                outv[0, r, t : t + 8, :] = outv[0, r, t : t + 8, :] - azim_t * inverse
                outv[1, r, t : t + 8, :] = outv[1, r, t : t + 8, :] + azim_r * inverse
            return carry

        lax.fori_loop(0, RAD, combine, 0)

    lax.fori_loop(0, RAD, stencils, 0)
    back = []
    for half in range(HALF):
        back += convert_and_apply(half)
    for half in range(HALF):
        finish(half)
    for copy in forward + back + halos:
        copy.wait_send()


def solution(mesh):
    lat_total = BAND * mesh.shape["lat"]
    spacing = math.pi / lat_total
    theta = (np.arange(lat_total, dtype=np.float32) + np.float32(0.5)) * np.float32(spacing)
    theta = theta.astype(np.float64)
    lat_scalars = np.concatenate([spacing / np.sin(theta), spacing * np.cos(theta) / np.sin(theta)]).astype(np.float32)
    radius = inner_radius + (np.arange(RAD) + 0.5) * spacing
    rad_scalars = np.zeros(128, np.float32)
    rad_scalars[3 : 3 + RAD] = radius
    rad_scalars[64 : 64 + RAD] = 1.0 / radius
    first, second, third = mode_tables()

    def on_device(magnetic, kept_modes):
        flat = magnetic.reshape(3, RAD * BAND, SEG)
        in_hbm = pl.BlockSpec(memory_space=pltpu.HBM)
        dma = pltpu.SemaphoreType.DMA
        return pl.pallas_call(
            functools.partial(kernel, lat_total),
            out_shape=jax.ShapeDtypeStruct(magnetic.shape, F32),
            in_specs=[in_hbm] * 8,
            out_specs=pl.BlockSpec(memory_space=pltpu.VMEM),
            scratch_shapes=[
                pltpu.SMEM((lat_total,), jnp.int32),
                pltpu.SMEM((2 * lat_total,), F32),
                pltpu.SMEM((128,), F32),
                pltpu.VMEM(first.shape, F32),
                pltpu.VMEM(second.shape, F32),
                pltpu.VMEM(third.shape, F32),
                pltpu.VMEM((2, 2 * PADR + RAD * BAND, SEG), F32),
                pltpu.VMEM((2, RAD + 6, BAND + 16, SEG), F32),
                pltpu.VMEM((BAND, ROWS, SEG), F32),
                pltpu.VMEM((HALF, AZ, ROWS, SEG), F32),
                pltpu.VMEM((HALF, 8, 2 * SEG, 2 * SEG), BF16),
                pltpu.VMEM((HALF, 8, 2 * SEG, 2 * SEG), BF16),
                pltpu.VMEM((16 * ROWS, 2 * SEG), BF16),
                pltpu.VMEM((16 * ROWS, 2 * SEG), BF16),
                pltpu.VMEM((8 * ROWS, 2 * SEG), F32),
                pltpu.VMEM((HALF, AZ, ROWS, SEG), F32),
                pltpu.VMEM((BAND * ROWS, SEG), F32),
                pltpu.VMEM((BAND, SEG), F32),
                pltpu.VMEM((HALF, AZ, SEG), F32),
                dma((3,)),
                dma((6,)),
                dma((HALF, AZ)),
                dma((HALF, AZ)),
                dma((HALF, AZ)),
                dma((HALF, AZ)),
                dma((2,)),
                dma((2,)),
            ],
            compiler_params=pltpu.CompilerParams(
                collective_id=0, has_side_effects=True, vmem_limit_bytes=40 * 1024 * 1024
            ),
        )(
            *(pltpu.with_memory_space_constraint(v, pltpu.HBM) for v in (
            magnetic, flat, kept_modes, jnp.asarray(lat_scalars), jnp.asarray(rad_scalars),
            jnp.asarray(first), jnp.asarray(second), jnp.asarray(third),
        )))

    return jax.shard_map(
        on_device,
        mesh=mesh,
        in_specs=(P(None, None, "lat", "azim"), P()),
        out_specs=P(None, None, "lat", "azim"),
        check_vma=False,
    )
```

```python
import functools
import math

import jax
import jax.numpy as jnp
import numpy as np
from jax import lax
from jax.experimental import pallas as pl
from jax.experimental.pallas import tpu as pltpu
from jax.sharding import PartitionSpec as P

MESH = pl.DeviceIdType.MESH
F32 = jnp.float32
BF16 = jnp.bfloat16

inner_radius = 0.7
stencil_coeffs = (-1.0 / 60.0, 3.0 / 20.0, -3.0 / 4.0, 0.0, 3.0 / 4.0, -3.0 / 20.0, 1.0 / 60.0)
OFFSETS = (-3, -2, -1, 1, 2, 3)

RAD = 32
BAND = 32
SEG = 128
AZ = 16
HALF = BAND // AZ
ROWS = 2 * RAD
PADR = 3 * BAND


def mode_tables():
    a = np.arange(128)[:, None]
    b = np.arange(32)[:, None]
    q = np.arange(SEG)[None, :]
    p = np.arange(AZ)[:, None]
    high = 2.0 * np.pi * ((a * q) % 64) / 64.0
    twist = 2.0 * np.pi * ((b * q) % 2048) / 2048.0
    low = 2.0 * np.pi * ((p * b.T) % 16) / 16.0
    first = np.concatenate([np.cos(high), np.sin(high)], axis=1)
    second = np.stack([np.cos(twist), np.sin(twist)])
    third = np.stack([np.cos(low), np.sin(low)])
    third = np.pad(third, ((0, 0), (0, 0), (0, 96)))
    return first.astype(np.float32), second.astype(np.float32), third.astype(np.float32)


def split(value):
    high = value.astype(BF16)
    return high, (value - high.astype(F32)).astype(BF16)


def send_order():
    order = []
    for chips in (4, 3, -3, 2, -2, 1, -1, 0):
        for core in (0, 1):
            order.append((chips, core))
    return order


def kernel(
    lat_total,
    x4, x3, kept_hbm, latsc_hbm, radsc_hbm, tab1_hbm, tab2_hbm, tab3_hbm,
    outv,
    kept, latsc, radsc, tab1, tab2, tab3, xs, ext, edge, beyond, xt, rcv, whi, wlo, fhi, flo, acc, ret, az, cot, gen,
    in_sem, small_sem, fsend, frecv, rsend, rrecv, hsend, hrecv, joined,
):
    lat = lax.axis_index("lat")
    me = lax.axis_index("azim")
    lats = lax.axis_size("lat")
    chip = me // 2
    core = me % 2
    north = (lat + lats - 1) % lats
    south = (lat + 1) % lats

    loads = [
        pltpu.make_async_copy(x3.at[0:2], xs.at[0:2, PADR : PADR + RAD * BAND, :], in_sem.at[0]),
        pltpu.make_async_copy(x4.at[0], ext.at[0, 3 : 3 + RAD, 8 : 8 + BAND, :], in_sem.at[1]),
        pltpu.make_async_copy(x4.at[2], ext.at[1, 3 : 3 + RAD, 8 : 8 + BAND, :], in_sem.at[2]),
        pltpu.make_async_copy(x3.at[2], xs.at[2, PADR : PADR + RAD * BAND, :], in_sem.at[3]),
    ]
    smalls = [
        pltpu.make_async_copy(kept_hbm, kept, small_sem.at[0]),
        pltpu.make_async_copy(latsc_hbm, latsc, small_sem.at[1]),
        pltpu.make_async_copy(radsc_hbm, radsc, small_sem.at[2]),
        pltpu.make_async_copy(tab1_hbm, tab1, small_sem.at[3]),
        pltpu.make_async_copy(tab2_hbm, tab2, small_sem.at[4]),
        pltpu.make_async_copy(tab3_hbm, tab3, small_sem.at[5]),
    ]
    for copy in loads + smalls:
        copy.start()

    barrier = pltpu.get_barrier_semaphore()

    @pl.when(me != 0)
    def _():
        for step in range(1, AZ):
            pl.semaphore_signal(barrier, inc=1, device_id={"azim": (me + step) % AZ}, device_id_type=MESH)

    @pl.when(lat > 0)
    def _():
        pl.semaphore_signal(barrier, inc=1, device_id={"lat": north}, device_id_type=MESH)

    @pl.when(lat < lats - 1)
    def _():
        pl.semaphore_signal(barrier, inc=1, device_id={"lat": south}, device_id_type=MESH)

    bands_beside = (lat + lats - 1) // lats + 1 - (lat + 1) // lats
    pl.semaphore_wait(barrier, AZ - 1 - (me + AZ - 1) // AZ + bands_beside)

    @pl.when(me == 0)
    def _():
        for step in range(1, AZ):
            pl.semaphore_signal(joined, inc=1, device_id={"azim": step}, device_id_type=MESH)

    loads[0].wait()

    peers = []
    for chips, flip in send_order():
        peer = ((chip + chips + 8) % 8) * 2 + (core + flip) % 2
        peers.append((peer, chips == 0 and flip == 0))
    def send_rows(half, row, peer):
        return pltpu.make_async_remote_copy(
            src_ref=xt.at[row],
            dst_ref=rcv.at[half, me],
            send_sem=fsend.at[half, peer],
            recv_sem=frecv.at[half, me],
            device_id={"azim": peer},
            device_id_type=MESH,
        )

    def forward_half(half, all_joined):
        sent = []
        for peer, own in peers:
            row = peer + AZ * half
            for c in range(2):
                for k in range(RAD // 8):
                    xt[row, c * RAD + 8 * k : c * RAD + 8 * k + 8, :] = xs[
                        c, pl.ds(PADR + 8 * k * BAND + row, 8, stride=BAND), :
                    ]
            if own:
                pltpu.make_async_copy(xt.at[row], rcv.at[half, me], frecv.at[half, me]).start()
            else:
                copy = send_rows(half, row, peer)
                if all_joined:
                    copy.start()
                else:
                    pl.when(peer != 0)(copy.start)
                sent.append(copy)
        return sent

    forward = forward_half(0, False)

    for copy in smalls:
        copy.wait()

    base = lat * BAND + me
    side = lax.broadcasted_iota(jnp.int32, (HALF * 32, 128), 0)
    a = lax.broadcasted_iota(jnp.int32, (HALF * 32, 128), 1)
    mode = 32 * a + side % 32
    first_half = side < 32
    limit = jnp.where(first_half, kept[base], kept[base + AZ])
    scale = jnp.where(first_half, latsc[base], latsc[base + AZ])
    weight = jnp.where(mode < limit, mode, 0).astype(F32) * (2.0 / (AZ * SEG)) * scale
    sums = jnp.dot(weight, tab1[...], precision=lax.Precision.HIGHEST, preferred_element_type=F32)
    for half in range(HALF):
        c_sum = sums[32 * half : 32 * half + 32, 0:SEG]
        s_sum = sums[32 * half : 32 * half + 32, SEG : 2 * SEG]
        tc = tab2[0]
        ts = tab2[1]
        zero = jnp.zeros((96, SEG), F32)
        real = jnp.concatenate([c_sum * tc - s_sum * ts, zero], axis=0)
        imag = jnp.concatenate([s_sum * tc + c_sum * ts, zero], axis=0)
        gen[half] = -(
            jnp.dot(tab3[0], imag, precision=lax.Precision.HIGHEST, preferred_element_type=F32)
            + jnp.dot(tab3[1], real, precision=lax.Precision.HIGHEST, preferred_element_type=F32)
        )
    for half in range(HALF):
        for p in range(AZ):
            pair = jnp.concatenate(
                [gen[half, (p + AZ - 1) % AZ : (p + AZ - 1) % AZ + 1, :], gen[half, p : p + 1, :]], axis=1
            )
            turned = pltpu.roll(jnp.broadcast_to(pair, (SEG, 2 * SEG)), 0, 1, stride=1, stride_axis=0)
            high, low = split(turned[:, SEG:])
            for tile in range(8):
                for i in range(2):
                    for j in range(2):
                        if (j - i - 2 * tile - p) % AZ == 0:
                            at = (half, tile, slice(SEG * i, SEG * i + SEG), slice(SEG * j, SEG * j + SEG))
                            whi[at] = high
                            wlo[at] = low

    @pl.when(me != 0)
    def _():
        pl.semaphore_wait(joined, 1)
        send_rows(0, 0, 0).start()

    forward += forward_half(1, True)

    loads[3].wait()
    for side, first_row in ((0, BAND - 3), (1, 0)):
        for i in range(3):
            for c in range(2):
                for k in range(RAD // 8):
                    edge[side, c, i, 8 * k : 8 * k + 8, :] = xs[
                        2 * c, pl.ds(PADR + 8 * k * BAND + first_row + i, 8, stride=BAND), :
                    ]
    halos = [
        pltpu.make_async_remote_copy(
            src_ref=edge.at[side],
            dst_ref=beyond.at[side],
            send_sem=hsend.at[side],
            recv_sem=hrecv.at[side],
            device_id={"lat": (south, north)[side]},
            device_id_type=MESH,
        )
        for side in range(2)
    ]
    pl.when(lat < lats - 1)(halos[0].start)
    pl.when(lat > 0)(halos[1].start)

    @pl.when(lat == 0)
    def _():
        beyond[0] = jnp.zeros((2, 3, RAD, SEG), F32)

    @pl.when(lat == lats - 1)
    def _():
        beyond[1] = jnp.zeros((2, 3, RAD, SEG), F32)

    loads[1].wait()
    loads[2].wait()

    zeros = jnp.zeros((3, BAND, SEG), F32)
    ext[1, 0:3, 8 : 8 + BAND, :] = zeros
    ext[1, 3 + RAD : 6 + RAD, 8 : 8 + BAND, :] = zeros
    xs[1, 0:PADR, :] = jnp.zeros((PADR, SEG), F32)
    xs[1, PADR + RAD * BAND : 2 * PADR + RAD * BAND, :] = jnp.zeros((PADR, SEG), F32)
    for t in range(BAND):
        cot[t : t + 1, :] = jnp.full((1, SEG), latsc[lat_total + lat * BAND + t], F32)

    def stencils(r, carry):
        for c in range(2):
            for i in range(3):
                ext[c, r + 3, 5 + i : 6 + i, :] = beyond[0, c, i, pl.ds(r, 1), :]
                ext[c, r + 3, 8 + BAND + i : 9 + BAND + i, :] = beyond[1, c, i, pl.ds(r, 1), :]
        inverse = radsc[64 + r]
        th_r = jnp.zeros((BAND, SEG), F32)
        th_p = jnp.zeros((BAND, SEG), F32)
        dr_t = jnp.zeros((BAND, SEG), F32)
        dr_p = jnp.zeros((BAND, SEG), F32)
        for o in OFFSETS:
            weight_o = stencil_coeffs[o + 3]
            th_r = th_r + weight_o * ext[0, r + 3, 8 + o : 8 + o + BAND, :]
            th_p = th_p + weight_o * ext[1, r + 3, 8 + o : 8 + o + BAND, :]
            scaled = weight_o * radsc[r + 3 + o]
            dr_t = dr_t + scaled * xs[1, pl.ds(pl.multiple_of((r + 3 + o) * BAND, BAND), BAND), :]
            dr_p = dr_p + scaled * ext[1, r + 3 + o, 8 : 8 + BAND, :]
        outv[0, r] = (th_p + cot[...] * ext[1, r + 3, 8 : 8 + BAND, :]) * inverse
        outv[1, r] = -dr_p * inverse
        outv[2, r] = (dr_t - th_r) * inverse
        return carry

    def convert_and_apply(half):
        for source in range(AZ):
            pltpu.make_async_copy(xt.at[0], rcv.at[half, source], frecv.at[half, source]).wait()
        for source in range(AZ):
            high, low = split(rcv[half, source])
            lanes = slice(SEG * (source % 2), SEG * (source % 2) + SEG)
            for wrap in range(2):
                rows = slice(ROWS * (source // 2 + 8 * wrap), ROWS * (source // 2 + 8 * wrap) + ROWS)
                fhi[rows, lanes] = high
                flo[rows, lanes] = low
        acc[...] = jnp.zeros_like(acc)

        def tile_step(tile, carry):
            rows = pl.ds(pl.multiple_of(tile * ROWS, ROWS), 8 * ROWS)
            f_high = fhi[rows, :]
            f_low = flo[rows, :]
            w_high = whi[half, tile]
            acc[...] += (
                jnp.dot(f_high, w_high, preferred_element_type=F32)
                + jnp.dot(f_high, wlo[half, tile], preferred_element_type=F32)
                + jnp.dot(f_low, w_high, preferred_element_type=F32)
            )
            return carry

        lax.fori_loop(0, 8, tile_step, 0)
        for block in range(AZ):
            ret[half, block] = acc[
                ROWS * (block // 2) : ROWS * (block // 2) + ROWS, SEG * (block % 2) : SEG * (block % 2) + SEG
            ]
        sent = []
        for peer, own in peers:
            target = az.at[pl.ds(pl.multiple_of((me + AZ * half) * ROWS, ROWS), ROWS), :]
            if own:
                pltpu.make_async_copy(ret.at[half, peer], target, rrecv.at[half, me]).start()
            else:
                copy = pltpu.make_async_remote_copy(
                    src_ref=ret.at[half, peer],
                    dst_ref=target,
                    send_sem=rsend.at[half, peer],
                    recv_sem=rrecv.at[half, me],
                    device_id={"azim": peer},
                    device_id_type=MESH,
                )
                copy.start()
                sent.append(copy)
        return sent

    def finish(half):
        for source in range(AZ):
            t = source + AZ * half
            pltpu.make_async_copy(
                ret.at[half, 0], az.at[t * ROWS : t * ROWS + ROWS, :], rrecv.at[half, source]
            ).wait()

        def combine(r, carry):
            inverse = radsc[64 + r]
            for k in range(AZ // 8):
                t = AZ * half + 8 * k
                azim_r = az[pl.ds(t * ROWS + r, 8, stride=ROWS), :]
                azim_t = az[pl.ds(t * ROWS + RAD + r, 8, stride=ROWS), :]
                outv[0, r, t : t + 8, :] = outv[0, r, t : t + 8, :] - azim_t * inverse
                outv[1, r, t : t + 8, :] = outv[1, r, t : t + 8, :] + azim_r * inverse
            return carry

        lax.fori_loop(0, RAD, combine, 0)

    back = []
    for half in range(HALF):
        back += convert_and_apply(half)
    pl.when(lat > 0)(halos[0].wait_recv)
    pl.when(lat < lats - 1)(halos[1].wait_recv)
    lax.fori_loop(0, RAD, stencils, 0)
    for half in range(HALF):
        finish(half)
    for copy in forward + back:
        copy.wait_send()
    pl.when(lat < lats - 1)(halos[0].wait_send)
    pl.when(lat > 0)(halos[1].wait_send)


def solution(mesh):
    lat_total = BAND * mesh.shape["lat"]
    spacing = math.pi / lat_total
    theta = (np.arange(lat_total, dtype=np.float32) + np.float32(0.5)) * np.float32(spacing)
    theta = theta.astype(np.float64)
    lat_scalars = np.concatenate([spacing / np.sin(theta), spacing * np.cos(theta) / np.sin(theta)]).astype(np.float32)
    radius = inner_radius + (np.arange(RAD) + 0.5) * spacing
    rad_scalars = np.zeros(128, np.float32)
    rad_scalars[3 : 3 + RAD] = radius
    rad_scalars[64 : 64 + RAD] = 1.0 / radius
    first, second, third = mode_tables()

    def on_device(magnetic, kept_modes):
        flat = magnetic.reshape(3, RAD * BAND, SEG)
        in_hbm = pl.BlockSpec(memory_space=pltpu.HBM)
        dma = pltpu.SemaphoreType.DMA
        return pl.pallas_call(
            functools.partial(kernel, lat_total),
            out_shape=jax.ShapeDtypeStruct(magnetic.shape, F32),
            in_specs=[in_hbm] * 8,
            out_specs=pl.BlockSpec(memory_space=pltpu.VMEM),
            scratch_shapes=[
                pltpu.SMEM((lat_total,), jnp.int32),
                pltpu.SMEM((2 * lat_total,), F32),
                pltpu.SMEM((128,), F32),
                pltpu.VMEM(first.shape, F32),
                pltpu.VMEM(second.shape, F32),
                pltpu.VMEM(third.shape, F32),
                pltpu.VMEM((3, 2 * PADR + RAD * BAND, SEG), F32),
                pltpu.VMEM((2, RAD + 6, BAND + 16, SEG), F32),
                pltpu.VMEM((2, 2, 3, RAD, SEG), F32),
                pltpu.VMEM((2, 2, 3, RAD, SEG), F32),
                pltpu.VMEM((BAND, ROWS, SEG), F32),
                pltpu.VMEM((HALF, AZ, ROWS, SEG), F32),
                pltpu.VMEM((HALF, 8, 2 * SEG, 2 * SEG), BF16),
                pltpu.VMEM((HALF, 8, 2 * SEG, 2 * SEG), BF16),
                pltpu.VMEM((16 * ROWS, 2 * SEG), BF16),
                pltpu.VMEM((16 * ROWS, 2 * SEG), BF16),
                pltpu.VMEM((8 * ROWS, 2 * SEG), F32),
                pltpu.VMEM((HALF, AZ, ROWS, SEG), F32),
                pltpu.VMEM((BAND * ROWS, SEG), F32),
                pltpu.VMEM((BAND, SEG), F32),
                pltpu.VMEM((HALF, AZ, SEG), F32),
                dma((4,)),
                dma((6,)),
                dma((HALF, AZ)),
                dma((HALF, AZ)),
                dma((HALF, AZ)),
                dma((HALF, AZ)),
                dma((2,)),
                dma((2,)),
                pltpu.SemaphoreType.REGULAR,
            ],
            compiler_params=pltpu.CompilerParams(
                collective_id=0, has_side_effects=True, vmem_limit_bytes=40 * 1024 * 1024
            ),
        )(
            *(pltpu.with_memory_space_constraint(v, pltpu.HBM) for v in (
            magnetic, flat, kept_modes, jnp.asarray(lat_scalars), jnp.asarray(rad_scalars),
            jnp.asarray(first), jnp.asarray(second), jnp.asarray(third),
        )))

    return jax.shard_map(
        on_device,
        mesh=mesh,
        in_specs=(P(None, None, "lat", "azim"), P()),
        out_specs=P(None, None, "lat", "azim"),
        check_vma=False,
    )
```

```python
import functools
import math

import jax
import jax.numpy as jnp
import numpy as np
from jax import lax
from jax.experimental import pallas as pl
from jax.experimental.pallas import tpu as pltpu
from jax.sharding import PartitionSpec as P

MESH = pl.DeviceIdType.MESH
F32 = jnp.float32
BF16 = jnp.bfloat16

inner_radius = 0.7
stencil_coeffs = (-1.0 / 60.0, 3.0 / 20.0, -3.0 / 4.0, 0.0, 3.0 / 4.0, -3.0 / 20.0, 1.0 / 60.0)
OFFSETS = (-3, -2, -1, 1, 2, 3)

RAD = 32
BAND = 32
SEG = 128
AZ = 16
HALF = BAND // AZ
ROWS = 2 * RAD
PADR = 3 * BAND


def mode_tables():
    a = np.arange(128)[:, None]
    b = np.arange(32)[:, None]
    q = np.arange(SEG)[None, :]
    p = np.arange(AZ)[:, None]
    high = 2.0 * np.pi * ((a * q) % 64) / 64.0
    twist = 2.0 * np.pi * ((b * q) % 2048) / 2048.0
    low = 2.0 * np.pi * ((p * b.T) % 16) / 16.0
    first = np.concatenate([np.cos(high), np.sin(high)], axis=1)
    second = np.stack([np.cos(twist), np.sin(twist)])
    third = np.stack([np.cos(low), np.sin(low)])
    third = np.pad(third, ((0, 0), (0, 0), (0, 96)))
    return first.astype(np.float32), second.astype(np.float32), third.astype(np.float32)


def split(value):
    high = value.astype(BF16)
    return high, (value - high.astype(F32)).astype(BF16)


def is_zero(value, bound):
    return 1 - (value + bound - 1) // bound


def send_order():
    order = []
    for chips in (0, 1, -1, 2, -2, 3, -3, 4):
        for core in (1, 0):
            order.append((chips, core))
    return order


def kernel(
    lat_total,
    x4, x3, kept_hbm, latsc_hbm, radsc_hbm, tab1_hbm, tab2_hbm, tab3_hbm,
    outv,
    kept, latsc, radsc, tab1, tab2, tab3, xs, ext, edge, beyond, xt, rcv, whi, wlo, fhi, flo, acc, ret, az, cot, gen,
    in_sem, small_sem, fsend, frecv, rsend, rrecv, hsend, hrecv, joined, beside,
):
    lat = lax.axis_index("lat")
    me = lax.axis_index("azim")
    lats = lax.axis_size("lat")
    chip = me // 2
    core = me % 2
    north = (lat + lats - 1) % lats
    south = (lat + 1) % lats

    loads = [
        pltpu.make_async_copy(x3.at[0:2], xs.at[0:2, PADR : PADR + RAD * BAND, :], in_sem.at[0]),
        pltpu.make_async_copy(x4.at[0], ext.at[0, 3 : 3 + RAD, 8 : 8 + BAND, :], in_sem.at[1]),
        pltpu.make_async_copy(x4.at[2], ext.at[1, 3 : 3 + RAD, 8 : 8 + BAND, :], in_sem.at[2]),
        pltpu.make_async_copy(x3.at[2], xs.at[2, PADR : PADR + RAD * BAND, :], in_sem.at[3]),
    ]
    smalls = [
        pltpu.make_async_copy(kept_hbm, kept, small_sem.at[0]),
        pltpu.make_async_copy(latsc_hbm, latsc, small_sem.at[1]),
        pltpu.make_async_copy(radsc_hbm, radsc, small_sem.at[2]),
        pltpu.make_async_copy(tab1_hbm, tab1, small_sem.at[3]),
        pltpu.make_async_copy(tab2_hbm, tab2, small_sem.at[4]),
        pltpu.make_async_copy(tab3_hbm, tab3, small_sem.at[5]),
    ]
    loads[0].start()

    barrier = pltpu.get_barrier_semaphore()

    @pl.when(me != 0)
    def _():
        for step in range(1, AZ):
            pl.semaphore_signal(barrier, inc=1, device_id={"azim": (me + step) % AZ}, device_id_type=MESH)

    greet_south = ((lat + 1) % 4 + 3) // 4 - is_zero(me, AZ) * is_zero(lat, lats)
    heard_north = (lat % 4 + 3) // 4 - is_zero(me, AZ) * is_zero((lat + lats - 1) % lats, lats)
    has_south = 1 - is_zero(lats - 1 - lat, lats)
    has_north = 1 - is_zero(lat, lats)
    greets_south = has_south * greet_south == 1
    waits_south = has_south * (1 - greet_south) == 1
    greets_north = has_north * (1 - heard_north) == 1
    waits_north = has_north * heard_north == 1

    @pl.when(greets_north)
    def _():
        pl.semaphore_signal(barrier, inc=1, device_id={"lat": north}, device_id_type=MESH)

    @pl.when(greets_south)
    def _():
        pl.semaphore_signal(barrier, inc=1, device_id={"lat": south}, device_id_type=MESH)

    for copy in loads[1:] + smalls:
        copy.start()
    pl.semaphore_wait(
        barrier, AZ - 1 - (me + AZ - 1) // AZ + has_south * (1 - greet_south) + has_north * heard_north
    )

    @pl.when(waits_north)
    def _():
        pl.semaphore_signal(beside.at[0], inc=1, device_id={"lat": north}, device_id_type=MESH)

    @pl.when(waits_south)
    def _():
        pl.semaphore_signal(beside.at[1], inc=1, device_id={"lat": south}, device_id_type=MESH)

    @pl.when(me == 0)
    def _():
        for step in range(1, AZ):
            pl.semaphore_signal(joined, inc=1, device_id={"azim": step}, device_id_type=MESH)

    loads[0].wait()

    peers = []
    for chips, flip in send_order():
        peer = ((chip + chips + 8) % 8) * 2 + (core + flip) % 2
        peers.append((peer, chips == 0 and flip == 0))
    def send_rows(half, row, peer):
        return pltpu.make_async_remote_copy(
            src_ref=xt.at[row],
            dst_ref=rcv.at[half, me],
            send_sem=fsend.at[half, peer],
            recv_sem=frecv.at[half, me],
            device_id={"azim": peer},
            device_id_type=MESH,
        )

    def fill(half, peer):
        row = peer + AZ * half
        for c in range(2):
            for k in range(RAD // 8):
                xt[row, c * RAD + 8 * k : c * RAD + 8 * k + 8, :] = xs[
                    c, pl.ds(PADR + 8 * k * BAND + row, 8, stride=BAND), :
                ]

    others = [peer for peer, own in peers if not own]
    forward = []
    for half in range(HALF):
        for peer in others:
            fill(half, peer)
            copy = send_rows(half, peer + AZ * half, peer)
            if half == 0:
                pl.when(peer != 0)(copy.start)
            forward.append(copy)
        fill(half, me)
        pltpu.make_async_copy(xt.at[me + AZ * half], rcv.at[half, me], frecv.at[half, me]).start()

    for copy in smalls:
        copy.wait()

    base = lat * BAND + me
    side = lax.broadcasted_iota(jnp.int32, (HALF * 32, 128), 0)
    a = lax.broadcasted_iota(jnp.int32, (HALF * 32, 128), 1)
    mode = 32 * a + side % 32
    first_half = side < 32
    limit = jnp.where(first_half, kept[base], kept[base + AZ])
    scale = jnp.where(first_half, latsc[base], latsc[base + AZ])
    weight = jnp.where(mode < limit, mode, 0).astype(F32) * (2.0 / (AZ * SEG)) * scale
    sums = jnp.dot(weight, tab1[...], precision=lax.Precision.HIGHEST, preferred_element_type=F32)
    for half in range(HALF):
        c_sum = sums[32 * half : 32 * half + 32, 0:SEG]
        s_sum = sums[32 * half : 32 * half + 32, SEG : 2 * SEG]
        tc = tab2[0]
        ts = tab2[1]
        zero = jnp.zeros((96, SEG), F32)
        real = jnp.concatenate([c_sum * tc - s_sum * ts, zero], axis=0)
        imag = jnp.concatenate([s_sum * tc + c_sum * ts, zero], axis=0)
        gen[half] = -(
            jnp.dot(tab3[0], imag, precision=lax.Precision.HIGHEST, preferred_element_type=F32)
            + jnp.dot(tab3[1], real, precision=lax.Precision.HIGHEST, preferred_element_type=F32)
        )
    for half in range(HALF):
        for p in range(AZ):
            pair = jnp.concatenate(
                [gen[half, (p + AZ - 1) % AZ : (p + AZ - 1) % AZ + 1, :], gen[half, p : p + 1, :]], axis=1
            )
            turned = pltpu.roll(jnp.broadcast_to(pair, (SEG, 2 * SEG)), 0, 1, stride=1, stride_axis=0)
            high, low = split(turned[:, SEG:])
            for tile in range(8):
                for i in range(2):
                    for j in range(2):
                        if (j - i - 2 * tile - p) % AZ == 0:
                            at = (half, tile, slice(SEG * i, SEG * i + SEG), slice(SEG * j, SEG * j + SEG))
                            whi[at] = high
                            wlo[at] = low

    @pl.when(me != 0)
    def _():
        pl.semaphore_wait(joined, 1)
        send_rows(0, 0, 0).start()

    for peer in others:
        send_rows(1, peer + AZ, peer).start()

    loads[3].wait()
    for side, first_row in ((0, BAND - 3), (1, 0)):
        for i in range(3):
            for c in range(2):
                for k in range(RAD // 8):
                    edge[side, c, i, 8 * k : 8 * k + 8, :] = xs[
                        2 * c, pl.ds(PADR + 8 * k * BAND + first_row + i, 8, stride=BAND), :
                    ]
    halos = [
        pltpu.make_async_remote_copy(
            src_ref=edge.at[side],
            dst_ref=beyond.at[side],
            send_sem=hsend.at[side],
            recv_sem=hrecv.at[side],
            device_id={"lat": (south, north)[side]},
            device_id_type=MESH,
        )
        for side in range(2)
    ]

    @pl.when(greets_south)
    def _():
        pl.semaphore_wait(beside.at[0], 1)

    pl.when(lat < lats - 1)(halos[0].start)

    @pl.when(greets_north)
    def _():
        pl.semaphore_wait(beside.at[1], 1)

    pl.when(lat > 0)(halos[1].start)

    @pl.when(lat == 0)
    def _():
        beyond[0] = jnp.zeros((2, 3, RAD, SEG), F32)

    @pl.when(lat == lats - 1)
    def _():
        beyond[1] = jnp.zeros((2, 3, RAD, SEG), F32)

    loads[1].wait()
    loads[2].wait()

    zeros = jnp.zeros((3, BAND, SEG), F32)
    ext[1, 0:3, 8 : 8 + BAND, :] = zeros
    ext[1, 3 + RAD : 6 + RAD, 8 : 8 + BAND, :] = zeros
    xs[1, 0:PADR, :] = jnp.zeros((PADR, SEG), F32)
    xs[1, PADR + RAD * BAND : 2 * PADR + RAD * BAND, :] = jnp.zeros((PADR, SEG), F32)
    for t in range(BAND):
        cot[t : t + 1, :] = jnp.full((1, SEG), latsc[lat_total + lat * BAND + t], F32)

    def stencils(r, carry):
        for c in range(2):
            for i in range(3):
                ext[c, r + 3, 5 + i : 6 + i, :] = beyond[0, c, i, pl.ds(r, 1), :]
                ext[c, r + 3, 8 + BAND + i : 9 + BAND + i, :] = beyond[1, c, i, pl.ds(r, 1), :]
        inverse = radsc[64 + r]
        th_r = jnp.zeros((BAND, SEG), F32)
        th_p = jnp.zeros((BAND, SEG), F32)
        dr_t = jnp.zeros((BAND, SEG), F32)
        dr_p = jnp.zeros((BAND, SEG), F32)
        for o in OFFSETS:
            weight_o = stencil_coeffs[o + 3]
            th_r = th_r + weight_o * ext[0, r + 3, 8 + o : 8 + o + BAND, :]
            th_p = th_p + weight_o * ext[1, r + 3, 8 + o : 8 + o + BAND, :]
            scaled = weight_o * radsc[r + 3 + o]
            dr_t = dr_t + scaled * xs[1, pl.ds(pl.multiple_of((r + 3 + o) * BAND, BAND), BAND), :]
            dr_p = dr_p + scaled * ext[1, r + 3 + o, 8 : 8 + BAND, :]
        outv[0, r] = (th_p + cot[...] * ext[1, r + 3, 8 : 8 + BAND, :]) * inverse
        outv[1, r] = -dr_p * inverse
        outv[2, r] = (dr_t - th_r) * inverse
        return carry

    def convert_and_apply(half):
        for source in range(AZ):
            pltpu.make_async_copy(xt.at[0], rcv.at[half, source], frecv.at[half, source]).wait()
        for source in range(AZ):
            high, low = split(rcv[half, source])
            lanes = slice(SEG * (source % 2), SEG * (source % 2) + SEG)
            for wrap in range(2):
                rows = slice(ROWS * (source // 2 + 8 * wrap), ROWS * (source // 2 + 8 * wrap) + ROWS)
                fhi[rows, lanes] = high
                flo[rows, lanes] = low
        acc[...] = jnp.zeros_like(acc)

        def tile_step(tile, carry):
            rows = pl.ds(pl.multiple_of(tile * ROWS, ROWS), 8 * ROWS)
            f_high = fhi[rows, :]
            f_low = flo[rows, :]
            w_high = whi[half, tile]
            acc[...] += (
                jnp.dot(f_high, w_high, preferred_element_type=F32)
                + jnp.dot(f_high, wlo[half, tile], preferred_element_type=F32)
                + jnp.dot(f_low, w_high, preferred_element_type=F32)
            )
            return carry

        lax.fori_loop(0, 8, tile_step, 0)
        for block in range(AZ):
            ret[half, block] = acc[
                ROWS * (block // 2) : ROWS * (block // 2) + ROWS, SEG * (block % 2) : SEG * (block % 2) + SEG
            ]
        sent = []
        for peer, own in peers:
            target = az.at[pl.ds(pl.multiple_of((me + AZ * half) * ROWS, ROWS), ROWS), :]
            if own:
                pltpu.make_async_copy(ret.at[half, peer], target, rrecv.at[half, me]).start()
            else:
                copy = pltpu.make_async_remote_copy(
                    src_ref=ret.at[half, peer],
                    dst_ref=target,
                    send_sem=rsend.at[half, peer],
                    recv_sem=rrecv.at[half, me],
                    device_id={"azim": peer},
                    device_id_type=MESH,
                )
                if half == 0:
                    copy.start()
                sent.append(copy)
        if half == HALF - 1:
            for target_chip in (0, 1, 7, 2, 6, 3, 5, 4):
                for peer in (2 * target_chip, 2 * target_chip + 1):
                    copy = pltpu.make_async_remote_copy(
                        src_ref=ret.at[half, peer],
                        dst_ref=az.at[pl.ds(pl.multiple_of((me + AZ * half) * ROWS, ROWS), ROWS), :],
                        send_sem=rsend.at[half, peer],
                        recv_sem=rrecv.at[half, me],
                        device_id={"azim": peer},
                        device_id_type=MESH,
                    )
                    pl.when(me != peer)(copy.start)
        return sent

    def finish(half):
        for source in range(AZ):
            t = source + AZ * half
            pltpu.make_async_copy(
                ret.at[half, 0], az.at[t * ROWS : t * ROWS + ROWS, :], rrecv.at[half, source]
            ).wait()

        def combine(r, carry):
            inverse = radsc[64 + r]
            for k in range(AZ // 8):
                t = AZ * half + 8 * k
                azim_r = az[pl.ds(t * ROWS + r, 8, stride=ROWS), :]
                azim_t = az[pl.ds(t * ROWS + RAD + r, 8, stride=ROWS), :]
                outv[0, r, t : t + 8, :] = outv[0, r, t : t + 8, :] - azim_t * inverse
                outv[1, r, t : t + 8, :] = outv[1, r, t : t + 8, :] + azim_r * inverse
            return carry

        lax.fori_loop(0, RAD, combine, 0)

    back = []
    for half in range(HALF):
        back += convert_and_apply(half)
    pl.when(lat > 0)(halos[0].wait_recv)
    pl.when(lat < lats - 1)(halos[1].wait_recv)
    lax.fori_loop(0, RAD, stencils, 0)
    for half in range(HALF):
        finish(half)
    for copy in forward + back:
        copy.wait_send()
    pl.when(lat < lats - 1)(halos[0].wait_send)
    pl.when(lat > 0)(halos[1].wait_send)


def solution(mesh):
    lat_total = BAND * mesh.shape["lat"]
    spacing = math.pi / lat_total
    theta = (np.arange(lat_total, dtype=np.float32) + np.float32(0.5)) * np.float32(spacing)
    theta = theta.astype(np.float64)
    lat_scalars = np.concatenate([spacing / np.sin(theta), spacing * np.cos(theta) / np.sin(theta)]).astype(np.float32)
    radius = inner_radius + (np.arange(RAD) + 0.5) * spacing
    rad_scalars = np.zeros(128, np.float32)
    rad_scalars[3 : 3 + RAD] = radius
    rad_scalars[64 : 64 + RAD] = 1.0 / radius
    first, second, third = mode_tables()

    def on_device(magnetic, kept_modes):
        flat = magnetic.reshape(3, RAD * BAND, SEG)
        in_hbm = pl.BlockSpec(memory_space=pltpu.HBM)
        dma = pltpu.SemaphoreType.DMA
        return pl.pallas_call(
            functools.partial(kernel, lat_total),
            out_shape=jax.ShapeDtypeStruct(magnetic.shape, F32),
            in_specs=[in_hbm] * 8,
            out_specs=pl.BlockSpec(memory_space=pltpu.VMEM),
            scratch_shapes=[
                pltpu.SMEM((lat_total,), jnp.int32),
                pltpu.SMEM((2 * lat_total,), F32),
                pltpu.SMEM((128,), F32),
                pltpu.VMEM(first.shape, F32),
                pltpu.VMEM(second.shape, F32),
                pltpu.VMEM(third.shape, F32),
                pltpu.VMEM((3, 2 * PADR + RAD * BAND, SEG), F32),
                pltpu.VMEM((2, RAD + 6, BAND + 16, SEG), F32),
                pltpu.VMEM((2, 2, 3, RAD, SEG), F32),
                pltpu.VMEM((2, 2, 3, RAD, SEG), F32),
                pltpu.VMEM((BAND, ROWS, SEG), F32),
                pltpu.VMEM((HALF, AZ, ROWS, SEG), F32),
                pltpu.VMEM((HALF, 8, 2 * SEG, 2 * SEG), BF16),
                pltpu.VMEM((HALF, 8, 2 * SEG, 2 * SEG), BF16),
                pltpu.VMEM((16 * ROWS, 2 * SEG), BF16),
                pltpu.VMEM((16 * ROWS, 2 * SEG), BF16),
                pltpu.VMEM((8 * ROWS, 2 * SEG), F32),
                pltpu.VMEM((HALF, AZ, ROWS, SEG), F32),
                pltpu.VMEM((BAND * ROWS, SEG), F32),
                pltpu.VMEM((BAND, SEG), F32),
                pltpu.VMEM((HALF, AZ, SEG), F32),
                dma((4,)),
                dma((6,)),
                dma((HALF, AZ)),
                dma((HALF, AZ)),
                dma((HALF, AZ)),
                dma((HALF, AZ)),
                dma((2,)),
                dma((2,)),
                pltpu.SemaphoreType.REGULAR,
                pltpu.SemaphoreType.REGULAR((2,)),
            ],
            compiler_params=pltpu.CompilerParams(
                collective_id=0, has_side_effects=True, vmem_limit_bytes=40 * 1024 * 1024
            ),
        )(
            *(pltpu.with_memory_space_constraint(v, pltpu.HBM) for v in (
            magnetic, flat, kept_modes, jnp.asarray(lat_scalars), jnp.asarray(rad_scalars),
            jnp.asarray(first), jnp.asarray(second), jnp.asarray(third),
        )))

    return jax.shard_map(
        on_device,
        mesh=mesh,
        in_specs=(P(None, None, "lat", "azim"), P()),
        out_specs=P(None, None, "lat", "azim"),
        check_vma=False,
    )
```
